32 devices in a mesh: dom: 16 (over z, y, x), row: 2 (over core).
Axes of the slice: x: 2, y: 2, z: 4, core: 2. Of those that a mesh axis runs over, the one named last changes fastest.
Arguments:
- right_side: float32 [16, 1024, 512], P('dom', 'row'), may hold values from -6 to 6
- lower_blocks: bfloat16 [16, 4, 1024, 1024], P('dom', None, 'row'), may hold values from -0.15625 to 0.15625
- upper_blocks: bfloat16 [16, 4, 1024, 1024], P('dom', None, 'row'), may hold values from -0.15625 to 0.15625
- final_blocks: bfloat16 [16, 1024, 1024], P('dom', 'row'), may hold values from -0.046875 to 0.046875
Outputs:
- solution: float32 [16, 1024, 512], P('dom', 'row')
The draws below stay inside these ranges and needn't reach their ends.
All inputs are finite; a program needn't handle non-finite values.
Results may differ from the reference program's by a relative error of at most 0.008.
Values may be sent and summed in bfloat16 or wider, within the bound.
No kernel may reach another device: no remote copies, remote signals or barrier semaphores. Data moves between devices by JAX's collectives and lax.ppermute only.
A program may use at most 64 MiB of HBM per device.

```python
import jax
import jax.numpy as jnp

W = 1024
RHS = 512
SLICES = 16
LEVELS = 4


def block_levels(own_key, dims, split, least, high):
    gain, own = 1.0, jax.random.fold_in(own_key, 6)
    for dim, blocks in split:
        steps = jnp.exp(jax.random.uniform(jax.random.fold_in(own, dim), (blocks,), jnp.float32, least / len(split), high / len(split)))
        gain = gain * jnp.repeat(steps, dims[dim] // blocks).reshape([-1 if axis == dim else 1 for axis in range(len(dims))])
    return gain


def noise(stream_key, extent, width, bound, shards=(), kind=jnp.bfloat16):
    values = width * jax.random.normal(stream_key, extent, jnp.float32)
    if shards:
        values = values * block_levels(stream_key, extent, shards, -0.22, 0.18)
    return jnp.clip(values, -bound, bound).astype(kind)


def setup_inputs(seed: int = 0) -> dict:
    key_list = jax.random.split(jax.random.key(seed), 5)
    return {
        "right_side": noise(key_list[0], (SLICES, W, RHS), 1.0, 6.0, ((0, 16), (1, 2)), jnp.float32),
        "lower_blocks": noise(key_list[1], (SLICES, LEVELS, W, W), (W * 25 // 16) ** -0.5, 0.15625, ((0, 16), (2, 2))),
        "upper_blocks": noise(key_list[2], (SLICES, LEVELS, W, W), (W * 25 // 16) ** -0.5, 0.15625, ((0, 16), (2, 2))),
        "final_blocks": noise(key_list[3], (SLICES, W, W), (W * 2 ** LEVELS) ** -0.5, 0.046875, ((0, 16), (1, 2))),
    }


def shifted(values, distance):
    zeros = jnp.zeros((distance,) + values.shape[1:], values.dtype)
    from_low = jnp.concatenate([zeros, values[:-distance]], 0)
    from_high = jnp.concatenate([values[distance:], zeros], 0)
    return from_low, from_high


def reference(right_side, lower_blocks, upper_blocks, final_blocks):
    current = right_side
    for level_index in range(LEVELS):
        distance = 2 ** level_index
        rounded = current.astype(jnp.bfloat16)
        from_low, from_high = shifted(rounded, distance)
        lower_term = jnp.einsum("pij,pjm->pim", lower_blocks[:, level_index].astype(jnp.float32), from_low.astype(jnp.float32))
        upper_term = jnp.einsum("pij,pjm->pim", upper_blocks[:, level_index].astype(jnp.float32), from_high.astype(jnp.float32))
        current = current + lower_term + upper_term
    final_state = current.astype(jnp.bfloat16)
    return jnp.einsum("pij,pjm->pim", final_blocks.astype(jnp.float32), final_state.astype(jnp.float32))
```

```python
import functools

import jax
import jax.numpy as jnp
from jax import lax
from jax.experimental import pallas as pl
from jax.experimental.pallas import tpu as pltpu
from jax.sharding import PartitionSpec as P


CHUNKS = 2
VMEM = pl.BlockSpec(memory_space=pltpu.VMEM)
HBM = pl.BlockSpec(memory_space=pltpu.HBM)
PARAMS = pltpu.CompilerParams(vmem_limit_bytes=8 * 2**20)


def in_vmem(value):
    return pltpu.with_memory_space_constraint(value, pltpu.MemorySpace.VMEM)


def in_hbm(value):
    return pltpu.with_memory_space_constraint(value, pltpu.MemorySpace.HBM)


def bit(level):
    return lax.bitwise_and(lax.shift_right_logical(lax.axis_index("dom"), level), 1)


def sides(half):
    core = lax.axis_index("row")
    return [pl.ds(pl.multiple_of(side * half, half), half) for side in (core, 1 - core)]


def plan(levels, count):
    uses = []
    for level in range(levels):
        if 2**level < count:
            uses.append((level, 1))
        if 2 ** (level + 1) < count:
            uses.append((level, 0))
    return uses


def load_kernel(uses, first, right, low, high, right_out, *rest):
    outs, sems = rest[:-1], rest[-1]
    copies = [pltpu.make_async_copy(right, right_out, sems.at[len(uses)])]
    copies[0].start()

    def target(index):
        return outs[0].at[index] if index < first else outs[1].at[index - first]

    for index, (level, partner) in enumerate(uses):
        @pl.when(bit(level) == partner)
        def _():
            pltpu.make_async_copy(low.at[level], target(index), sems.at[index]).start()

        @pl.when(bit(level) != partner)
        def _():
            pltpu.make_async_copy(high.at[level], target(index), sems.at[index]).start()

    for index, (level, _) in enumerate(uses):
        pltpu.make_async_copy(low.at[level], target(index), sems.at[index]).wait()
    copies[0].wait()


def load(right, low, high, uses, first):
    block = low.shape[1:]
    return pl.pallas_call(
        functools.partial(load_kernel, uses, first),
        in_specs=[HBM] * 3,
        out_specs=[VMEM] * 3,
        out_shape=[
            pltpu.VMEM(right.shape, right.dtype),
            pltpu.VMEM((first, *block), low.dtype),
            pltpu.VMEM((len(uses) - first, *block), low.dtype),
        ],
        scratch_shapes=[pltpu.SemaphoreType.DMA((len(uses) + 1,))],
        compiler_params=PARAMS,
        cost_estimate=pl.CostEstimate(flops=0, bytes_accessed=2 * len(uses) * block[0] * block[1], transcendentals=0),
        name="load",
    )(in_hbm(right), in_hbm(low), in_hbm(high))


def take_kernel(chunk, mine, theirs, state, rounded):
    half = mine.shape[0]
    width = state.shape[1]
    columns = pl.ds(pl.multiple_of((lax.axis_index("row") * CHUNKS + chunk) * width, width), width)
    for source, place in zip((mine, theirs), sides(half)):
        value = source[:, columns]
        state[place, :] = value
        rounded[place, :] = value.astype(jnp.bfloat16)


def take(mine, theirs, chunk, width):
    rows = 2 * mine.shape[0]
    return pl.pallas_call(
        functools.partial(take_kernel, chunk),
        in_specs=[VMEM] * 2,
        out_specs=[VMEM] * 2,
        out_shape=[pltpu.VMEM((rows, width), jnp.float32), pltpu.VMEM((rows, width), jnp.bfloat16)],
        compiler_params=PARAMS,
        cost_estimate=pl.CostEstimate(flops=0, bytes_accessed=10 * rows * width, transcendentals=0),
        name="take",
    )(in_vmem(mine), in_vmem(theirs))


def step_kernel(use, index, distance, count, state, operand, own, other, *outputs):
    level, partner = use

    def write(place, total):
        for output in outputs:
            output[place, :] = total.astype(output.dtype)

    def add():
        for blocks, place in zip((own, other), sides(own.shape[1])):
            write(
                place,
                state[place, :] + jnp.dot(blocks[index], operand[...], preferred_element_type=jnp.float32),
            )

    if partner:
        add()
    else:
        place = lax.axis_index("dom")
        source = jnp.where(bit(level) == 1, place + distance, place - distance)
        inside = (source >= 0) & (source < count)
        pl.when(inside)(add)

        @pl.when(jnp.logical_not(inside))
        def _():
            write(slice(None), state[...])


def step(use, index, distance, count, state, operand, own, other, kinds):
    rows, width = state.shape
    return pl.pallas_call(
        functools.partial(step_kernel, use, index, distance, count),
        in_specs=[VMEM] * 4,
        out_specs=[VMEM] * len(kinds),
        out_shape=[pltpu.VMEM((rows, width), kind) for kind in kinds],
        compiler_params=PARAMS,
        cost_estimate=pl.CostEstimate(
            flops=2 * rows * rows * width, bytes_accessed=2 * rows * rows + 12 * rows * width, transcendentals=0
        ),
        name=f"step{use[0]}{use[1]}",
    )(in_vmem(state), in_vmem(operand), in_vmem(own), in_vmem(other))


def finish_kernel(blocks, *refs):
    out = refs[-1]
    core = lax.axis_index("row")
    count = len(refs) // 2
    width = refs[0].shape[1]
    for index in range(2 * count):
        side = core if index < count else 1 - core
        column = pl.multiple_of((side * count + index % count) * width, width)
        out[:, pl.ds(column, width)] = jnp.dot(blocks[...], refs[index][...], preferred_element_type=jnp.float32)


def finish(blocks, mine, theirs):
    half, rows = blocks.shape
    width = mine[0].shape[1]
    total = 2 * len(mine) * width
    return pl.pallas_call(
        finish_kernel,
        in_specs=[VMEM] * (1 + 2 * len(mine)),
        out_specs=VMEM,
        out_shape=jax.ShapeDtypeStruct((half, total), jnp.float32),
        compiler_params=PARAMS,
        cost_estimate=pl.CostEstimate(
            flops=2 * half * rows * total, bytes_accessed=2 * half * rows + 4 * half * total, transcendentals=0
        ),
        name="finish",
    )(blocks, *mine, *theirs)


def body(right_side, lower_blocks, upper_blocks, final_blocks):
    count = lax.axis_size("dom")
    levels = lower_blocks.shape[1]
    width = right_side.shape[2] // (2 * CHUNKS)
    uses = plan(levels, count)

    def send(value, target, idle):
        moves = [(p, target(p) if 0 <= target(p) < count else idle(p)) for p in range(count)]
        return lax.ppermute(value, "dom", moves)

    swap = functools.partial(lax.ppermute, axis_name="row", perm=[(0, 1), (1, 0)])
    theirs = swap(right_side[0])
    mine, own_first, own_rest = load(right_side[0], lower_blocks[0], upper_blocks[0], uses, 2)
    theirs, own_first, own_rest = lax.optimization_barrier((theirs, own_first, own_rest))
    other_first = swap(own_first)
    other_rest = swap(own_rest)

    def blocks(index):
        return (index, own_first, other_first) if index < 2 else (index - 2, own_rest, other_rest)

    results = []
    for chunk in range(CHUNKS):
        state, rounded = take(mine, theirs, chunk, width)
        for index, (level, partner) in enumerate(uses):
            distance = 2**level
            if partner:
                arrived = send(rounded, lambda p: p ^ distance, None)
            elif 4 * distance < count:
                arrived = send(
                    arrived, lambda p: p - 2 * distance if p & distance else p + 2 * distance, lambda p: p ^ distance
                )
            else:
                arrived = send(rounded, lambda p: p + distance if p & distance else p - distance, lambda p: p ^ 1)
            half_way = partner and 2 * distance < count
            last = index == len(uses) - 1
            kinds = [jnp.float32] if half_way else ([jnp.bfloat16] if last else [jnp.float32, jnp.bfloat16])
            number, own, other = blocks(index)
            outs = step((level, partner), number, distance, count, state, arrived, own, other, kinds)
            state, rounded = outs[0], rounded if half_way else outs[-1]
        results.append(rounded)
    return finish(final_blocks[0], results, [swap(value) for value in results])[None]


def solution(mesh):
    in_specs = (
        P("dom", "row", None),
        P("dom", None, "row", None),
        P("dom", None, "row", None),
        P("dom", "row", None),
    )
    out_specs = P("dom", "row", None)
    return jax.shard_map(body, mesh=mesh, in_specs=in_specs, out_specs=out_specs, check_vma=False)
```

```python
import functools

import jax
import jax.numpy as jnp
from jax import lax
from jax.experimental import pallas as pl
from jax.experimental.pallas import tpu as pltpu
from jax.sharding import PartitionSpec as P


CHUNKS = 2
VMEM = pl.BlockSpec(memory_space=pltpu.VMEM)
HBM = pl.BlockSpec(memory_space=pltpu.HBM)
PARAMS = pltpu.CompilerParams(vmem_limit_bytes=8 * 2**20)


def in_vmem(value):
    return pltpu.with_memory_space_constraint(value, pltpu.MemorySpace.VMEM)


def in_hbm(value):
    return pltpu.with_memory_space_constraint(value, pltpu.MemorySpace.HBM)


def bit(level):
    return lax.bitwise_and(lax.shift_right_logical(lax.axis_index("dom"), level), 1)


def sides(half):
    core = lax.axis_index("row")
    return [pl.ds(pl.multiple_of(side * half, half), half) for side in (core, 1 - core)]


def plan(levels, count):
    uses = []
    for level in range(levels):
        if 2**level < count:
            uses.append((level, 1))
        if 2 ** (level + 1) < count:
            uses.append((level, 0))
    return uses


def copy_blocks(uses, first, low, high, outs, sems):
    def target(index):
        return outs[0].at[index] if index < first else outs[1].at[index - first]

    for index, (level, partner) in enumerate(uses):
        @pl.when(bit(level) == partner)
        def _():
            pltpu.make_async_copy(low.at[level], target(index), sems.at[index]).start()

        @pl.when(bit(level) != partner)
        def _():
            pltpu.make_async_copy(high.at[level], target(index), sems.at[index]).start()

    for index, (level, _) in enumerate(uses):
        pltpu.make_async_copy(low.at[level], target(index), sems.at[index]).wait()


def open_kernel(right, mine, away, short, sem):
    copy = pltpu.make_async_copy(right, mine, sem)
    copy.start()
    copy.wait()
    half = away.shape[1]
    value = mine[:, pl.ds(pl.multiple_of((1 - lax.axis_index("row")) * half, half), half)]
    away[...] = value
    short[...] = value.astype(jnp.bfloat16)


def open_call(right):
    half = right.shape[1] // 2
    return pl.pallas_call(
        open_kernel,
        in_specs=[HBM],
        out_specs=[VMEM] * 3,
        out_shape=[
            pltpu.VMEM(right.shape, right.dtype),
            pltpu.VMEM((right.shape[0], half), right.dtype),
            pltpu.VMEM((right.shape[0], half), jnp.bfloat16),
        ],
        scratch_shapes=[pltpu.SemaphoreType.DMA],
        compiler_params=PARAMS,
        cost_estimate=pl.CostEstimate(flops=0, bytes_accessed=4 * right.shape[0] * half, transcendentals=0),
        name="open",
    )(in_hbm(right))


def load_kernel(uses, first, low, high, after, *rest):
    copy_blocks(uses, first, low, high, rest[:-1], rest[-1])


def load(low, high, after, uses, first):
    block = low.shape[1:]
    return pl.pallas_call(
        functools.partial(load_kernel, uses, first),
        in_specs=[HBM] * 2 + [VMEM],
        out_specs=[VMEM] * 2,
        out_shape=[
            pltpu.VMEM((first, *block), low.dtype),
            pltpu.VMEM((len(uses) - first, *block), low.dtype),
        ],
        scratch_shapes=[pltpu.SemaphoreType.DMA((len(uses),))],
        compiler_params=PARAMS,
        cost_estimate=pl.CostEstimate(flops=0, bytes_accessed=2 * len(uses) * block[0] * block[1], transcendentals=0),
        name="load",
    )(in_hbm(low), in_hbm(high), in_vmem(after))


def columns_of(chunk, width):
    return pl.ds(pl.multiple_of((lax.axis_index("row") * CHUNKS + chunk) * width, width), width)


def take_kernel(chunk, mine, theirs, rounded):
    width = rounded.shape[1]
    here, there = sides(mine.shape[0])
    rounded[here, :] = mine[:, columns_of(chunk, width)].astype(jnp.bfloat16)
    rounded[there, :] = theirs[:, chunk * width : (chunk + 1) * width]


def take(mine, theirs, chunk, width):
    rows = 2 * mine.shape[0]
    return pl.pallas_call(
        functools.partial(take_kernel, chunk),
        in_specs=[VMEM] * 2,
        out_specs=VMEM,
        out_shape=pltpu.VMEM((rows, width), jnp.bfloat16),
        compiler_params=PARAMS,
        cost_estimate=pl.CostEstimate(flops=0, bytes_accessed=8 * rows * width, transcendentals=0),
        name="take",
    )(in_vmem(mine), in_vmem(theirs))


def inside(level, count):
    place, distance = lax.axis_index("dom"), 2**level
    source = jnp.where(bit(level) == 1, place + distance, place - distance)
    return (source >= 0) & (source < count)


def turn_kernel(works, first, count, chunk, sizes, groups, *refs):
    parts, operands, _ = sizes
    states, refs = refs[:parts], refs[parts:]
    given, refs = refs[:operands], refs[operands:]
    pairs = {group: refs[2 * place : 2 * place + 2] for place, group in enumerate(groups)}
    state, *outs = refs[2 * len(groups) :]
    width = state.shape[1]

    def read(side, place):
        if parts == 1:
            return state[place, :]
        if side == 0:
            return states[0][:, columns_of(chunk, width)]
        return states[1][:, chunk * width : (chunk + 1) * width]

    def add(terms, fresh):
        for side, place in enumerate(sides(state.shape[0] // 2)):
            total = read(side, place)
            for use, operand in terms:
                total += jnp.dot(
                    pairs[use >= first][side][use - first * (use >= first)],
                    given[operand][...],
                    preferred_element_type=jnp.float32,
                )
            state[place, :] = total
            for out in fresh:
                out[place, :] = total.astype(out.dtype)

    def work(terms, results):
        fresh = [out for out, result in zip(outs, results) if result == "new"]
        far = [term for term in terms if term[0] % 2]
        if far:
            near = [term for term in terms if not term[0] % 2]
            there = inside(far[0][0] // 2, count)
            pl.when(there)(lambda: add(terms, fresh))
            pl.when(jnp.logical_not(there))(lambda: add(near, fresh))
        elif terms or fresh:
            add(terms, fresh)
        for out, result in zip(outs, results):
            if result not in ("new", None):
                out[...] = given[result][...]

    if works[0] == works[1]:
        work(*works[0])
    else:
        for core in range(2):
            pl.when(lax.axis_index("row") == core)(functools.partial(work, *works[core]))


def turn(works, states, given, blocks, first, count, chunk):
    rows, width = given[0].shape
    sends = len(works[0][1])
    groups = sorted({use >= first for terms, _ in works for use, _ in terms})
    inputs = (*states, *given, *(value for group in groups for value in blocks[group]))
    terms = max(len(work[0]) for work in works)
    outs = pl.pallas_call(
        functools.partial(turn_kernel, works, first, count, chunk, (len(states), len(given), sends), groups),
        in_specs=[VMEM] * len(inputs),
        out_specs=[VMEM] * (1 + sends),
        out_shape=[pltpu.VMEM((rows, width), jnp.float32)] + [pltpu.VMEM((rows, width), jnp.bfloat16)] * sends,
        input_output_aliases={0: 0} if len(states) == 1 else {},
        compiler_params=PARAMS,
        cost_estimate=pl.CostEstimate(
            flops=2 * rows * rows * width * terms,
            bytes_accessed=2 * rows * rows * terms + 12 * rows * width,
            transcendentals=0,
        ),
        name="turn",
    )(*(in_vmem(value) for value in inputs))
    return outs[0], outs[1:]


def copy_kernel(ones, zeros, out):
    @pl.when(lax.axis_index("row") == 0)
    def _():
        out[...] = zeros[...]

    @pl.when(lax.axis_index("row") == 1)
    def _():
        out[...] = ones[...]


def choose(zeros, ones):
    return pl.pallas_call(
        copy_kernel,
        in_specs=[VMEM] * 2,
        out_specs=VMEM,
        out_shape=pltpu.VMEM(zeros.shape, zeros.dtype),
        compiler_params=PARAMS,
        cost_estimate=pl.CostEstimate(flops=0, bytes_accessed=4 * zeros.size, transcendentals=0),
        name="choose",
    )(in_vmem(ones), in_vmem(zeros))


def finish_kernel(blocks, *refs):
    out = refs[-1]
    core = lax.axis_index("row")
    count = len(refs) // 2
    width = refs[0].shape[1]
    for index in range(2 * count):
        side = core if index < count else 1 - core
        column = pl.multiple_of((side * count + index % count) * width, width)
        out[:, pl.ds(column, width)] = jnp.dot(blocks[...], refs[index][...], preferred_element_type=jnp.float32)


def finish(blocks, mine, theirs):
    half, rows = blocks.shape
    width = mine[0].shape[1]
    total = 2 * len(mine) * width
    return pl.pallas_call(
        finish_kernel,
        in_specs=[VMEM] * (1 + 2 * len(mine)),
        out_specs=VMEM,
        out_shape=jax.ShapeDtypeStruct((half, total), jnp.float32),
        compiler_params=PARAMS,
        cost_estimate=pl.CostEstimate(
            flops=2 * half * rows * total, bytes_accessed=2 * half * rows + 4 * half * total, transcendentals=0
        ),
        name="finish",
    )(blocks, *mine, *theirs)


def target(kind, level):
    distance = 2**level
    if kind == "near":
        return lambda p: p ^ distance
    if kind == "far":
        return lambda p: p + distance if p & distance else p - distance
    if kind == "idle":
        return lambda p: p ^ 1
    sign = -1 if kind == "onward" else 1
    return lambda p: p + 2 * sign * distance if p & distance else p - 2 * sign * distance


def routes(moves, count):
    pairs = []
    for core, (kind, level) in enumerate(moves):
        to = target(kind, level)
        for p in range(count):
            if 0 <= to(p) < count:
                pairs.append((2 * p + core, 2 * to(p) + core))
            elif kind == "far":
                pairs.append((2 * p + core, 2 * (p ^ 1) + core))
            else:
                pairs.append((2 * p + core, 2 * p + 1 - core))
    return pairs


def solve(right_side, lower_blocks, upper_blocks, final_blocks):
    count = lax.axis_size("dom")
    levels = lower_blocks.shape[1]
    width = right_side.shape[2] // (2 * CHUNKS)
    uses = plan(levels, count)

    def send(moves, value):
        return lax.ppermute(value, ("dom", "row"), routes(moves, count))

    def swap(value):
        return lax.ppermute(value, "row", [(0, 1), (1, 0)])

    mine, away, short = open_call(right_side[0])
    theirs_short = swap(short)
    takes = []
    for chunk in range(CHUNKS):
        takes.append(take(mine, theirs_short, chunk, width))
    own = load(lower_blocks[0], upper_blocks[0], takes[1], uses, 2)
    theirs = swap(away)
    other = [swap(value) for value in own]
    blocks = list(zip(own, other))

    def chain(chunk):
        def run(works, states, given):
            return turn(works, states, given, blocks, 2, count, chunk)

        own_values = takes[chunk]
        near = send([("near", 0)] * 2, own_values)
        outgoing = choose(near, own_values)
        state, _ = run([([(0, 0)], [])] * 2, (mine, theirs), [near])
        middle = levels - 2
        for k in range(middle):
            moved = send([("onward", k), ("ahead", k)], outgoing)
            results = ["new"] * 2 if k else ["new"]
            relay = [0, 1] if k else [0]
            state, outs = run([([(2 * k + 1, 0)], results), ([], relay)], (state,), [moved, own_values])
            arrived = send([("near", k + 1), ("near", k)], outs[0])
            given = [arrived]
            if k:
                beside = ("far", k + 1) if k + 1 == middle else ("idle", 0)
                given.append(send([beside, ("near", k)], outs[1]))
            terms = [(2 * k + 1, 0)] + ([(2 * k, 1)] if k else [])
            if k + 1 < middle:
                state, outs = run([([], [0, None]), (terms, ["new", "new"])], (state,), given)
                outgoing, own_values = outs
                state, _ = run([([(2 * k + 2, 0)], []), ([], [])], (state,), [arrived])
            else:
                state, outs = run([([(2 * k + 2, 0), (2 * k + 3, 1)], ["new"]), (terms, ["new"])], (state,), given)
        one = send([("near", levels - 1), ("near", middle)], outs[0])
        two = send([("idle", 0), ("far", middle)], outs[0])
        last = 2 * levels - 2
        state, outs = run(
            [([(last, 0)], ["new"]), ([(2 * middle, 0), (2 * middle + 1, 1)], ["new"])], (state,), [one, two]
        )
        three = send([("idle", 0), ("near", levels - 1)], outs[0])
        state, outs = run([([], [1]), ([(last, 0)], ["new"])], (state,), [three, outs[0]])
        return outs[0]

    results = [chain(chunk) for chunk in range(CHUNKS)]
    swapped = [swap(value) for value in results]
    return finish(final_blocks[0], results, swapped)[None]


def solution(mesh):
    in_specs = (
        P("dom", "row", None),
        P("dom", None, "row", None),
        P("dom", None, "row", None),
        P("dom", "row", None),
    )
    out_specs = P("dom", "row", None)
    return jax.shard_map(solve, mesh=mesh, in_specs=in_specs, out_specs=out_specs, check_vma=False)
```

```python
import functools

import jax
import jax.numpy as jnp
from jax import lax
from jax.experimental import pallas as pl
from jax.experimental.pallas import tpu as pltpu
from jax.sharding import PartitionSpec as P


CHUNKS = 2
VMEM = pl.BlockSpec(memory_space=pltpu.VMEM)
HBM = pl.BlockSpec(memory_space=pltpu.HBM)
PARAMS = pltpu.CompilerParams(vmem_limit_bytes=8 * 2**20)


def in_vmem(value):
    return pltpu.with_memory_space_constraint(value, pltpu.MemorySpace.VMEM)


def in_hbm(value):
    return pltpu.with_memory_space_constraint(value, pltpu.MemorySpace.HBM)


def bit(level):
    return lax.bitwise_and(lax.shift_right_logical(lax.axis_index("dom"), level), 1)


def sides(half):
    core = lax.axis_index("row")
    return [pl.ds(pl.multiple_of(side * half, half), half) for side in (core, 1 - core)]


def plan(levels, count):
    uses = []
    for level in range(levels):
        if 2**level < count:
            uses.append((level, 1))
        if 2 ** (level + 1) < count:
            uses.append((level, 0))
    return uses


def copy_blocks(uses, first, low, high, outs, sems):
    def target(index):
        return outs[0].at[index] if index < first else outs[1].at[index - first]

    for index, (level, partner) in enumerate(uses):
        @pl.when(bit(level) == partner)
        def _():
            pltpu.make_async_copy(low.at[level], target(index), sems.at[index]).start()

        @pl.when(bit(level) != partner)
        def _():
            pltpu.make_async_copy(high.at[level], target(index), sems.at[index]).start()

    for index, (level, _) in enumerate(uses):
        pltpu.make_async_copy(low.at[level], target(index), sems.at[index]).wait()


def open_kernel(right, mine, away, short, sem):
    copy = pltpu.make_async_copy(right, mine, sem)
    copy.start()
    copy.wait()
    half = away.shape[1]
    value = mine[:, pl.ds(pl.multiple_of((1 - lax.axis_index("row")) * half, half), half)]
    away[...] = value
    short[...] = value.astype(jnp.bfloat16)


def open_call(right):
    half = right.shape[1] // 2
    return pl.pallas_call(
        open_kernel,
        in_specs=[HBM],
        out_specs=[VMEM] * 3,
        out_shape=[
            pltpu.VMEM(right.shape, right.dtype),
            pltpu.VMEM((right.shape[0], half), right.dtype),
            pltpu.VMEM((right.shape[0], half), jnp.bfloat16),
        ],
        scratch_shapes=[pltpu.SemaphoreType.DMA],
        compiler_params=PARAMS,
        cost_estimate=pl.CostEstimate(flops=0, bytes_accessed=4 * right.shape[0] * half, transcendentals=0),
        name="open",
    )(in_hbm(right))


def load_kernel(uses, first, low, high, ends, *rest):
    outs, (ends_out, sems, sem) = rest[:2], rest[2:]
    copy = pltpu.make_async_copy(ends, ends_out, sem)
    copy.start()
    copy_blocks(uses, first, low, high, outs, sems)
    copy.wait()


def load(low, high, ends, uses, first):
    block = low.shape[1:]
    outs = pl.pallas_call(
        functools.partial(load_kernel, uses, first),
        in_specs=[HBM] * 3,
        out_specs=[VMEM] * 3,
        out_shape=[
            pltpu.VMEM((first, *block), low.dtype),
            pltpu.VMEM((len(uses) - first, *block), low.dtype),
            pltpu.VMEM(ends.shape, ends.dtype),
        ],
        scratch_shapes=[pltpu.SemaphoreType.DMA((len(uses),)), pltpu.SemaphoreType.DMA],
        compiler_params=PARAMS,
        cost_estimate=pl.CostEstimate(flops=0, bytes_accessed=2 * len(uses) * block[0] * block[1], transcendentals=0),
        name="load",
    )(in_hbm(low), in_hbm(high), in_hbm(ends))
    return outs[:2], outs[2]


def columns_of(chunk, width):
    return pl.ds(pl.multiple_of((lax.axis_index("row") * CHUNKS + chunk) * width, width), width)


def take_kernel(chunk, mine, theirs, rounded):
    width = rounded.shape[1]
    here, there = sides(mine.shape[0])
    rounded[here, :] = mine[:, columns_of(chunk, width)].astype(jnp.bfloat16)
    rounded[there, :] = theirs[:, chunk * width : (chunk + 1) * width]


def take(mine, theirs, chunk, width):
    rows = 2 * mine.shape[0]
    return pl.pallas_call(
        functools.partial(take_kernel, chunk),
        in_specs=[VMEM] * 2,
        out_specs=VMEM,
        out_shape=pltpu.VMEM((rows, width), jnp.bfloat16),
        compiler_params=PARAMS,
        cost_estimate=pl.CostEstimate(flops=0, bytes_accessed=8 * rows * width, transcendentals=0),
        name="take",
    )(in_vmem(mine), in_vmem(theirs))


def inside(level, count):
    place, distance = lax.axis_index("dom"), 2**level
    source = jnp.where(bit(level) == 1, place + distance, place - distance)
    return (source >= 0) & (source < count)


def turn_kernel(works, first, count, chunk, sizes, groups, *refs):
    parts, operands, _ = sizes
    states, refs = refs[:parts], refs[parts:]
    given, refs = refs[:operands], refs[operands:]
    pairs = {group: refs[2 * place : 2 * place + 2] for place, group in enumerate(groups)}
    state, *outs = refs[2 * len(groups) :]
    width = state.shape[1]

    def read(side, place):
        if parts == 1:
            return state[place, :]
        if side == 0:
            return states[0][:, columns_of(chunk, width)]
        return states[1][:, chunk * width : (chunk + 1) * width]

    def add(terms, fresh):
        for side, place in enumerate(sides(state.shape[0] // 2)):
            total = read(side, place)
            for use, operand in terms:
                total += jnp.dot(
                    pairs[use >= first][side][use - first * (use >= first)],
                    given[operand][...],
                    preferred_element_type=jnp.float32,
                )
            state[place, :] = total
            for out in fresh:
                out[place, :] = total.astype(out.dtype)

    def work(terms, results):
        fresh = [out for out, result in zip(outs, results) if result == "new"]
        far = [term for term in terms if term[0] % 2]
        if far:
            near = [term for term in terms if not term[0] % 2]
            there = inside(far[0][0] // 2, count)
            pl.when(there)(lambda: add(terms, fresh))
            pl.when(jnp.logical_not(there))(lambda: add(near, fresh))
        elif terms or fresh or parts == 2:
            add(terms, fresh)
        for out, result in zip(outs, results):
            if result not in ("new", None):
                out[...] = given[result][...]

    if works[0] == works[1]:
        work(*works[0])
    else:
        for core in range(2):
            pl.when(lax.axis_index("row") == core)(functools.partial(work, *works[core]))


def turn(works, states, given, blocks, first, count, chunk):
    rows, width = given[0].shape
    sends = len(works[0][1])
    groups = sorted({use >= first for terms, _ in works for use, _ in terms})
    inputs = (*states, *given, *(value for group in groups for value in blocks[group]))
    terms = max(len(work[0]) for work in works)
    outs = pl.pallas_call(
        functools.partial(turn_kernel, works, first, count, chunk, (len(states), len(given), sends), groups),
        in_specs=[VMEM] * len(inputs),
        out_specs=[VMEM] * (1 + sends),
        out_shape=[pltpu.VMEM((rows, width), jnp.float32)] + [pltpu.VMEM((rows, width), jnp.bfloat16)] * sends,
        input_output_aliases={0: 0} if len(states) == 1 else {},
        compiler_params=PARAMS,
        cost_estimate=pl.CostEstimate(
            flops=2 * rows * rows * width * terms,
            bytes_accessed=2 * rows * rows * terms + 12 * rows * width,
            transcendentals=0,
        ),
        name="turn",
    )(*(in_vmem(value) for value in inputs))
    return outs[0], outs[1:]


def copy_kernel(ones, zeros, out):
    @pl.when(lax.axis_index("row") == 0)
    def _():
        out[...] = zeros[...]

    @pl.when(lax.axis_index("row") == 1)
    def _():
        out[...] = ones[...]


def choose(zeros, ones):
    return pl.pallas_call(
        copy_kernel,
        in_specs=[VMEM] * 2,
        out_specs=VMEM,
        out_shape=pltpu.VMEM(zeros.shape, zeros.dtype),
        compiler_params=PARAMS,
        cost_estimate=pl.CostEstimate(flops=0, bytes_accessed=4 * zeros.size, transcendentals=0),
        name="choose",
    )(in_vmem(ones), in_vmem(zeros))


def close_kernel(places, final, width, *refs):
    blocks, values = refs[0], refs[1 : 1 + len(places)]
    core = lax.axis_index("row")
    if final is None:
        refs[-1][...] = jnp.dot(blocks[...], values[0][...], preferred_element_type=jnp.float32)
        return
    out, kept, sems = refs[-3:]
    copies = []

    def put(source, place):
        side, chunk = place
        side = core if side == 0 else 1 - core
        columns = pl.ds(pl.multiple_of((side * CHUNKS + chunk) * width, width), width)
        copies.append(pltpu.make_async_copy(source, out.at[:, columns], sems.at[len(copies)]))
        copies[-1].start()

    if final:
        put(refs[1 + len(places)], final)
    for index, place in enumerate(places):
        kept[index] = jnp.dot(blocks[...], values[index][...], preferred_element_type=jnp.float32)
        put(kept.at[index], place)
    for copy in copies:
        copy.wait()


def close(blocks, places, values, done=None, held=None, final=()):
    half, rows = blocks.shape
    width = values[0].shape[1]
    inputs = [in_vmem(blocks), *(in_vmem(value) for value in values)]
    specs = [VMEM] * len(inputs)
    if held is not None:
        inputs.append(in_vmem(held))
        specs.append(VMEM)
    if done is not None:
        inputs.append(in_hbm(done))
        specs.append(HBM)
    scratch = []
    if final is None:
        shape, out_spec = pltpu.VMEM((half, width), jnp.float32), VMEM
    else:
        shape, out_spec = pltpu.HBM((half, 2 * CHUNKS * width), jnp.float32), HBM
        scratch = [pltpu.VMEM((len(places), half, width), jnp.float32), pltpu.SemaphoreType.DMA((len(places) + 1,))]
    return pl.pallas_call(
        functools.partial(close_kernel, places, final, width),
        in_specs=specs,
        out_specs=out_spec,
        out_shape=shape,
        scratch_shapes=scratch,
        input_output_aliases={len(inputs) - 1: 0} if done is not None else {},
        compiler_params=PARAMS,
        cost_estimate=pl.CostEstimate(
            flops=2 * half * rows * width * len(places), bytes_accessed=4 * half * width, transcendentals=0
        ),
        name="close",
    )(*inputs)


LONG = (True, True)


def target(kind, level):
    distance = 2**level
    if kind == "near":
        return lambda p: p ^ distance
    if kind == "far":
        return lambda p: p + distance if p & distance else p - distance
    if kind == "idle":
        return lambda p: p ^ 1
    sign = -1 if kind == "onward" else 1
    return lambda p: p + 2 * sign * distance if p & distance else p - 2 * sign * distance


def routes(moves, count, crossed=False):
    pairs = []
    paired = [kind for kind, _ in moves] == ["onward", "ahead"]
    for core, (kind, level) in enumerate(moves):
        to = target(kind, level)
        sender = 1 - core if crossed else core
        for p in range(count):
            if 0 <= to(p) < count:
                pairs.append((2 * p + sender, 2 * to(p) + core))
            elif kind == "far":
                pairs.append((2 * p + sender, 2 * (p ^ 1) + core))
            elif paired:
                pairs.append((2 * p + sender, 2 * p + 1 - core))
            else:
                pairs.append((2 * p + sender, 2 * (to(p) % count if LONG[kind == "onward"] else p ^ 2**level) + core))
    return pairs


def solve(right_side, lower_blocks, upper_blocks, final_blocks):
    count = lax.axis_size("dom")
    levels = lower_blocks.shape[1]
    width = right_side.shape[2] // (2 * CHUNKS)
    uses = plan(levels, count)

    def send(moves, value, crossed=False):
        return lax.ppermute(value, ("dom", "row"), routes(moves, count, crossed))

    def swap(value):
        return lax.ppermute(value, "row", [(0, 1), (1, 0)])

    mine, away, short = open_call(right_side[0])
    theirs_short = swap(short)
    takes = []
    for chunk in range(CHUNKS):
        takes.append(take(mine, theirs_short, chunk, width))
    own, ends = load(lower_blocks[0], upper_blocks[0], final_blocks[0], uses, 2)
    theirs = swap(away)
    other = [swap(value) for value in own]
    blocks = list(zip(own, other))

    def chain(chunk):
        def run(works, states, given):
            return turn(works, states, given, blocks, 2, count, chunk)

        near = send([("near", 0), ("ahead", 0)], takes[chunk])
        outgoing = choose(near, takes[chunk])
        state, _ = run([([(0, 0)], []), ([], [])], (mine, theirs), [near])
        middle = levels - 2
        moved = send([("onward", 0), ("near", 0)], outgoing)
        for k in range(middle):
            last = k + 1 == middle
            far = ([(2 * k + 1, 0)], ["new"] * (2 if k or last else 1))
            if k == 0:
                other_core = ([(0, 0)], [1] + [None] * last)
            else:
                other_core = ([], [0, 1])
            state, outs = run([far, other_core], (state,), [moved, outgoing if k else near])
            given = [send([("near", k + 1), ("near", k)], outs[0])]
            if k or last:
                beside = [("far", k + 1) if last else ("idle", 0), ("near", k) if k else ("idle", 0)]
                given.append(send(beside, outs[1]))
            terms = [(2 * k + 1, 0)] + ([(2 * k, 1)] if k else [])
            if not last:
                state, (outgoing,) = run([([], [0]), (terms, ["new"])], (state,), given)
                moved = send([("onward", k + 1), ("ahead", k + 1)], outgoing)
                state, _ = run([([(2 * k + 2, 0)], []), ([], [])], (state,), given[:1])
            else:
                first = ([(2 * k + 2, 0), (2 * k + 3, 1)], ["new"])
                state, outs = run([first, (terms, ["new"])], (state,), given)
        one = send([("near", levels - 1), ("near", middle)], outs[0])
        two = send([("idle", 0), ("far", middle)], outs[0])
        last = 2 * levels - 2
        state, outs = run(
            [([(last, 0)], ["new"]), ([(2 * middle, 0), (2 * middle + 1, 1)], ["new"])], (state,), [one, two]
        )
        three = send([("idle", 0), ("near", levels - 1)], outs[0])
        state, outs = run([([], [1]), ([(last, 0)], ["new"])], (state,), [three, outs[0]])
        return outs[0]

    results = [chain(chunk) for chunk in range(CHUNKS)]
    swapped = [swap(value) for value in results]
    out = close(ends, [(0, 0), (1, 0)], [results[0], swapped[0]])
    held = close(ends, [(0, 1)], [results[1]], final=None)
    return close(ends, [(1, 1)], [swapped[1]], out, held, (0, 1))[None]


def solution(mesh):
    in_specs = (
        P("dom", "row", None),
        P("dom", None, "row", None),
        P("dom", None, "row", None),
        P("dom", "row", None),
    )
    out_specs = P("dom", "row", None)
    return jax.shard_map(solve, mesh=mesh, in_specs=in_specs, out_specs=out_specs, check_vma=False)
```
